512 devices in a mesh: ctx: 64 (over z, y), head: 8 (over x, core).
Axes of the slice: x: 4, y: 4, z: 16, core: 2. Of those that a mesh axis runs over, the one named last changes fastest.
Arguments:
- lin_queries: bfloat16 [16384, 8192], P('ctx', 'head'), may hold values from -6 to 6
- lin_keys: bfloat16 [16384, 8192], P('ctx', 'head'), may hold values from -6 to 6
- lin_values: bfloat16 [16384, 8192], P('ctx', 'head'), may hold values from -21 to 21
- log_decay: float32 [16384, 64], P('ctx', 'head'), may hold values from -1 to 0
- lin_gate: bfloat16 [16384, 8192], P('ctx', 'head'), may hold values from -6 to 6
- norm_gain: float32 [8192], P('head'), may hold values from 0.1 to 1.9
- soft_queries: bfloat16 [16384, 8192], P('ctx', 'head'), may hold values from -6 to 6
- slab_keys: bfloat16 [16384, 1024], P('ctx', 'head'), may hold values from -6 to 6
- slab_values: bfloat16 [16384, 1024], P('ctx', 'head'), may hold values from -6 to 6
- cache_keys: bfloat16 [65536, 1024], P('ctx', 'head'), may hold values from -6 to 6
- cache_values: bfloat16 [65536, 1024], P('ctx', 'head'), may hold values from -6 to 6
- block_lists: int32 [128, 16], replicated, may hold values from 0 to 511, as said below
- live_counts: int32 [128], replicated, may hold values from 2 to 16
Outputs:
- lin_out: bfloat16 [16384, 8192], P('ctx', 'head')
- soft_out: bfloat16 [16384, 8192], P('ctx', 'head')
The draws below stay inside these ranges and needn't reach their ends.
Inputs may be any that keep to these rules, and one draw needn't show every extreme that they name: `block_lists`: cache block g lies on ctx index g // 8. One list names 16 blocks on 16 different ctx indices, and all lists of the 2 query blocks of one ctx index name at most one block of any one ctx index. Entries from live_counts on are not read.
All inputs are finite; a program needn't handle non-finite values.
Results may differ from the reference program's by a relative error of at most 0.0046.
Values may be sent and summed in bfloat16 or wider, within the bound.
A program may use at most 128 MiB of HBM per device.

```python
import jax
import jax.numpy as jnp
from jax import lax

QUERY_HEADS = 64
KV_HEADS = 8
HD = 128
TOK_DEV = 256
BLOCK = 128
NSEL = 16
SLAB_TOKENS = 16384
CACHE = 65536
QB_DEV = 2
BLK_DEV = 8
QBLOCKS = 128
CBLOCKS = 512
RSET = 24
QF = 8192
KF = 1024


def draw_lin_values(key, part):
    head_place = (jnp.arange(QF) // HD).astype(jnp.float32) / max(QUERY_HEADS - 1, 1)
    base = jnp.clip(jax.random.normal(jax.random.fold_in(key, 31), (SLAB_TOKENS, QF), jnp.float32), -6.0, 6.0)
    spread = 0.5 * jnp.log(3.0)
    head_scale = jnp.exp(spread * head_place)
    return (base * head_scale[None, :]).astype(jnp.bfloat16)


def draw_log_decay(key, part):
    fast_share = 0.5
    fast = jax.random.uniform(jax.random.fold_in(key, 41), (QUERY_HEADS,), jnp.float32) < fast_share
    slow_rate = jnp.exp(jax.random.uniform(jax.random.fold_in(key, 42), (QUERY_HEADS,), jnp.float32, jnp.log(0.1), jnp.log(0.5))) / SLAB_TOKENS
    fast_rate = jax.random.uniform(jax.random.fold_in(key, 43), (QUERY_HEADS,), jnp.float32, 1.0 / 50.0, 1.0 / 30.0)
    rate = jnp.where(fast, fast_rate, slow_rate)
    segments = SLAB_TOKENS // TOK_DEV
    seg_factor = jnp.exp(jax.random.uniform(jax.random.fold_in(key, 44), (segments, QUERY_HEADS), jnp.float32, jnp.log(0.6), jnp.log(1.5)))
    jitter = jax.random.uniform(jax.random.fold_in(key, 45), (SLAB_TOKENS, QUERY_HEADS), jnp.float32, 0.5, 1.5)
    steady_level = -rate[None, :] * seg_factor[jnp.arange(SLAB_TOKENS) // TOK_DEV] * jitter
    spike_position = jax.random.randint(jax.random.fold_in(key, 46), (2, QUERY_HEADS), 0, SLAB_TOKENS)
    layer_depth = jax.random.uniform(jax.random.fold_in(key, 47), (2, QUERY_HEADS), jnp.float32, 0.22, 0.69)
    device_positions = jnp.arange(SLAB_TOKENS)[:, None]
    spike_events = jnp.where(device_positions == spike_position[0][None, :], layer_depth[0][None, :], 0.0) + jnp.where(device_positions == spike_position[1][None, :], layer_depth[1][None, :], 0.0)
    return (steady_level - spike_events).astype(jnp.float32)


def draw_soft_queries(key, part):
    base = jnp.clip(jax.random.normal(jax.random.fold_in(key, 51), (SLAB_TOKENS, QF), jnp.float32), -6.0, 6.0)
    return base.astype(jnp.bfloat16)


def draw_cache_keys(key, part):
    base = jnp.clip(jax.random.normal(jax.random.fold_in(key, 61), (CACHE, KF), jnp.float32), -6.0, 6.0)
    return base.astype(jnp.bfloat16)


def request_sets(base_key, device_count):
    hotness = jax.random.randint(jax.random.fold_in(base_key, 11), (device_count,), 0, 5)
    noise = jax.random.randint(jax.random.fold_in(base_key, 12), (device_count, device_count), 0, 65536)
    owner_ids = jnp.arange(device_count, dtype=jnp.int32)
    scores = (hotness[None, :] * 24576 + noise) * device_count + owner_ids[None, :]
    unused, owners = lax.top_k(scores, RSET)
    spots = jax.random.randint(jax.random.fold_in(base_key, 13), (device_count, RSET), 0, BLK_DEV)
    return (owners * BLK_DEV + spots).astype(jnp.int32)


def draw_block_lists(key, part):
    device_count = QBLOCKS // QB_DEV
    choices_all = request_sets(key, device_count)
    picker = jax.random.randint(jax.random.fold_in(key, 14), (QBLOCKS, RSET), 0, 65536)
    picker = picker * RSET + jnp.arange(RSET, dtype=jnp.int32)[None, :]
    unused, chosen = lax.top_k(picker, NSEL)
    own_sets = choices_all[jnp.arange(QBLOCKS) // QB_DEV]
    return jnp.take_along_axis(own_sets, chosen, axis=1).astype(jnp.int32)


def draw_live_counts(key, part):
    device_count = QBLOCKS // QB_DEV
    heavy = jax.random.randint(jax.random.fold_in(key, 21), (device_count,), 0, 8) == 0
    light = jax.random.randint(jax.random.fold_in(key, 22), (device_count,), 1, 3) * (NSEL // 4)
    levels = jnp.where(heavy, NSEL, light)
    trimmed = jax.random.randint(jax.random.fold_in(key, 23), (QBLOCKS,), 0, 2) * (NSEL // 8)
    counts_all = jnp.maximum(1, levels[jnp.arange(QBLOCKS) // QB_DEV] - trimmed)
    forced = jax.random.randint(jax.random.fold_in(key, 24), (), 0, QBLOCKS)
    counts_all = jnp.where(jnp.arange(QBLOCKS) == forced, NSEL, counts_all)
    return counts_all.astype(jnp.int32)


def block_levels(stream_key, extent, cuts, low, top_value):
    def one(dim, blocks):
        steps = jax.random.uniform(jax.random.fold_in(jax.random.fold_in(stream_key, 6), dim), (blocks,), jnp.float32, low / len(cuts), top_value / len(cuts))
        return jnp.repeat(jnp.exp(steps), extent[dim] // blocks).reshape((-1,) + (1,) * (len(extent) - dim - 1))

    gain = one(*cuts[0])
    for cut in cuts[1:]:
        gain = gain * one(*cut)
    return gain


def centred(key, shape, scale, bound, cuts=(), kind=jnp.bfloat16):
    array = jax.random.normal(key, shape, jnp.float32) * scale
    if len(cuts) > 0:
        array = block_levels(key, shape, cuts, -0.22, 0.18) * array
    return jnp.clip(array, min=-bound, max=bound).astype(kind)


def setup_inputs(seed: int = 0) -> dict:
    key_list = jax.random.split(jax.random.key(seed), 14)
    lin_queries = centred(key_list[0], (SLAB_TOKENS, QF), 1.0, 6.0, ((0, 64), (1, 8)))
    lin_keys = centred(key_list[1], (SLAB_TOKENS, QF), 1.0, 6.0, ((0, 64), (1, 8)))
    lin_values = draw_lin_values(jax.random.fold_in(key_list[13], 71), 0)
    log_decay = draw_log_decay(jax.random.fold_in(key_list[13], 71), 0)
    lin_gate = centred(key_list[4], (SLAB_TOKENS, QF), 1.0, 6.0, ((0, 64), (1, 8)))
    norm_gain = jnp.clip(1.0 + 0.18 * jax.random.normal(key_list[5], (QF,), jnp.float32), 0.1, 1.9)
    soft_queries = draw_soft_queries(jax.random.fold_in(key_list[13], 71), 0)
    slab_keys = centred(key_list[7], (SLAB_TOKENS, KF), 1.0, 6.0, ((0, 64), (1, 8)))
    slab_values = centred(key_list[8], (SLAB_TOKENS, KF), 1.0, 6.0, ((0, 64), (1, 8)))
    cache_keys = draw_cache_keys(jax.random.fold_in(key_list[13], 71), 0)
    cache_values = centred(key_list[10], (CACHE, KF), 1.0, 6.0, ((0, 64), (1, 8)))
    block_lists = draw_block_lists(jax.random.fold_in(key_list[13], 71), 0)
    live_counts = draw_live_counts(jax.random.fold_in(key_list[13], 71), 0)
    return {"lin_queries": lin_queries, "lin_keys": lin_keys, "lin_values": lin_values, "log_decay": log_decay, "lin_gate": lin_gate, "norm_gain": norm_gain, "soft_queries": soft_queries, "slab_keys": slab_keys, "slab_values": slab_values, "cache_keys": cache_keys, "cache_values": cache_values, "block_lists": block_lists, "live_counts": live_counts}


def lightning_part(lin_queries, lin_keys, lin_values, log_decay, lin_gate, norm_gain):
    segments = SLAB_TOKENS // TOK_DEV
    act_queries = jax.nn.silu(lin_queries.astype(jnp.float32)).astype(jnp.bfloat16)
    act_keys = jax.nn.silu(lin_keys.astype(jnp.float32)).astype(jnp.bfloat16)
    act_queries = act_queries.reshape(segments, TOK_DEV, QUERY_HEADS, HD)
    act_keys = act_keys.reshape(segments, TOK_DEV, QUERY_HEADS, HD)
    values_all = lin_values.reshape(segments, TOK_DEV, QUERY_HEADS, HD)
    decays = log_decay.reshape(segments, TOK_DEV, QUERY_HEADS)
    causal = jnp.arange(TOK_DEV)[:, None] >= jnp.arange(TOK_DEV)[None, :]

    def segment_step(entering, pieces):
        seg_queries, seg_keys, seg_values, seg_decay = pieces
        running = jnp.cumsum(seg_decay, axis=0)
        seg_total = running[-1]
        flipped = running.T
        gaps = flipped[:, :, None] - flipped[:, None, :]
        weight = jnp.where(causal[None], jnp.exp(jnp.minimum(gaps, 0.0)), 0.0)
        scores = jnp.einsum('thd,shd->hts', seg_queries.astype(jnp.float32), seg_keys.astype(jnp.float32))
        lin_scores = (scores * weight).astype(jnp.bfloat16)
        intra = jnp.einsum('hts,shd->thd', lin_scores.astype(jnp.float32), seg_values.astype(jnp.float32))
        inter = jnp.exp(running)[:, :, None] * jnp.einsum('thd,hde->the', seg_queries.astype(jnp.float32), entering, precision=lax.Precision.HIGHEST)
        fade = jnp.exp(seg_total[None, :] - running)
        seg_state = jnp.einsum('shd,she->hde', seg_keys.astype(jnp.float32) * fade[:, :, None], seg_values.astype(jnp.float32), precision=lax.Precision.HIGHEST)
        leaving = jnp.exp(seg_total)[:, None, None] * entering + seg_state
        return (leaving, intra + inter)
    start_state = jnp.zeros((QUERY_HEADS, HD, HD), jnp.float32)
    unused, lin_attn = lax.scan(segment_step, start_state, (act_queries, act_keys, values_all, decays))
    lin_attn = lin_attn.reshape(SLAB_TOKENS, QUERY_HEADS * HD)
    squares = lax.optimization_barrier(jnp.mean(lin_attn * lin_attn, axis=1))
    scaling = lax.rsqrt(squares + 1e-06)
    gated = lin_attn * scaling[:, None] * norm_gain[None, :] * jax.nn.sigmoid(lin_gate.astype(jnp.float32))
    return gated.astype(jnp.bfloat16)

def softmax_part(soft_queries, slab_keys, slab_values, cache_keys, cache_values, block_lists, live_counts):
    group_size = QUERY_HEADS // KV_HEADS
    cache_key_blocks = cache_keys.reshape(CBLOCKS, BLOCK, KV_HEADS, HD)
    cache_value_blocks = cache_values.reshape(CBLOCKS, BLOCK, KV_HEADS, HD)
    inverse_root = 1.0 / HD ** 0.5

    def one_block(block_index):
        listed = block_lists[block_index]
        live_count = live_counts[block_index]
        chosen_keys = cache_key_blocks[listed].reshape(NSEL * BLOCK, KV_HEADS, HD)
        chosen_values = cache_value_blocks[listed].reshape(NSEL * BLOCK, KV_HEADS, HD)
        seg_start = (block_index // QB_DEV * TOK_DEV).astype(jnp.int32)
        own_keys = lax.dynamic_slice_in_dim(slab_keys, seg_start, TOK_DEV, 0).reshape(TOK_DEV, KV_HEADS, HD)
        own_values = lax.dynamic_slice_in_dim(slab_values, seg_start, TOK_DEV, 0).reshape(TOK_DEV, KV_HEADS, HD)
        query_start = (block_index * BLOCK).astype(jnp.int32)
        queries = lax.dynamic_slice_in_dim(soft_queries, query_start, BLOCK, 0).reshape(BLOCK, KV_HEADS, group_size, HD)
        all_keys = jnp.concatenate([chosen_keys, own_keys], axis=0).astype(jnp.float32)
        all_values = jnp.concatenate([chosen_values, own_values], axis=0).astype(jnp.float32)
        scores = jnp.einsum('tkgd,skd->kgts', queries.astype(jnp.float32), all_keys) * inverse_root
        cache_live = jnp.arange(NSEL * BLOCK) // BLOCK < live_count
        positions = block_index % QB_DEV * BLOCK + jnp.arange(BLOCK)
        causal = jnp.arange(TOK_DEV)[None, :] <= positions[:, None]
        allowed = jnp.concatenate([jnp.broadcast_to(cache_live[None, :], (BLOCK, NSEL * BLOCK)), causal], axis=1)
        scores = jnp.where(allowed[None, None], scores, -1e+30)
        highest = lax.optimization_barrier(jnp.max(scores, axis=3, keepdims=True))
        weights = jnp.exp(scores - highest)
        totals = lax.optimization_barrier(jnp.sum(weights, axis=3))
        soft_weights = weights.astype(jnp.bfloat16)
        mixed = jnp.einsum('kgts,skd->tkgd', soft_weights.astype(jnp.float32), all_values)
        normed = mixed / jnp.transpose(totals, (2, 0, 1))[:, :, :, None]
        return normed.astype(jnp.bfloat16).reshape(BLOCK, QUERY_HEADS * HD)
    outputs = lax.map(one_block, jnp.arange(QBLOCKS, dtype=jnp.int32))
    return outputs.reshape(SLAB_TOKENS, QUERY_HEADS * HD)

def reference(lin_queries, lin_keys, lin_values, log_decay, lin_gate, norm_gain, soft_queries, slab_keys, slab_values, cache_keys, cache_values, block_lists, live_counts):
    lin_out = lightning_part(lin_queries, lin_keys, lin_values, log_decay, lin_gate, norm_gain)
    soft_out = softmax_part(soft_queries, slab_keys, slab_values, cache_keys, cache_values, block_lists, live_counts)
    return (lin_out, soft_out)
```

```python
import functools
import math

import jax
import jax.numpy as jnp
from jax import lax
from jax.experimental import pallas as pl
from jax.experimental.pallas import tpu as pltpu
from jax.sharding import PartitionSpec as P

QUERY_HEADS = 64
HD = 128
BLOCK = 128
NZ = 16
NY = 4
MESH = pl.DeviceIdType.MESH
VMEM_LIMIT = 60 * 1024 * 1024


def exchange_kernel(sel_ref, ck_ref, cv_ref, st_ref, fin_ref, ent_ref, scr):
    bufs_p, bufs_m, far, stage = scr["bufs_p"], scr["bufs_m"], scr["far"], scr["stage"]
    me = lax.axis_index("ctx")
    z = me // NY
    y = me % NY

    def at(zz, yy):
        return {"ctx": zz * NY + yy}

    def zplus(k):
        return (z + k) % NZ

    def yplus(k):
        return (y + k) % NY

    barrier = pltpu.get_barrier_semaphore()
    for r in range(1, NY):
        pl.semaphore_signal(barrier, inc=1, device_id=at(z, yplus(r)), device_id_type=MESH)
    for r in range(1, NZ):
        pl.semaphore_signal(barrier, inc=1, device_id=at(zplus(r), y), device_id_type=MESH)
    pl.semaphore_wait(barrier, NY - 1 + NZ - 1)

    sends = []

    def copy(src, dst, ssem, rsem, where):
        made = pltpu.make_async_remote_copy(
            src_ref=src,
            dst_ref=dst,
            send_sem=ssem,
            recv_sem=rsem,
            device_id=where,
            device_id_type=MESH,
        )
        sends.append(made)
        return made

    yall, rz, tz, zr, zt = scr["yall"], scr["rz"], scr["tz"], scr["zr"], scr["zt"]
    ez, er, eq, pre = scr["ez"], scr["er"], scr["eq"], scr["pre"]
    ya = []
    for r in range(1, NY):
        ya.append(
            copy(
                st_ref.at[yplus(r)],
                yall.at[y],
                scr["ya_s"].at[r - 1],
                scr["ya_r"].at[r - 1],
                at(z, yplus(r)),
            )
        )
        ya[-1].start()
    def part(ref, c):
        return ref.at[c // 2, pl.ds(4 * (c % 2), 4)]

    def home(c):
        return (ck_ref, cv_ref)[c // 2].at[pl.ds(4 * (c % 2), 4)]

    def buffer(sign, d):
        if d == NZ // 2:
            return far
        return (bufs_p if sign > 0 else bufs_m)[d - 1]

    def travels(sign, d, c):
        return d < NZ // 2 or (d == NZ // 2 and (c < 2) == (sign > 0))

    ring = {}

    def send_ring(sign, d, c):
        if not travels(sign, d, c):
            return
        src = home(c) if d == 1 else part(buffer(sign, d - 1), c)
        k = 0 if sign > 0 else 1
        made = copy(
            src,
            part(buffer(sign, d), c),
            scr["ring_s"].at[k, d - 1, c],
            scr["ring_r"].at[k, d - 1, c],
            at(zplus(1 if sign > 0 else NZ - 1), y),
        )
        ring[sign, d, c] = made
        made.start()

    for c in range(4):
        send_ring(1, 1, c)
        send_ring(-1, 1, c)

    picks = []

    def pick(n, offset, load):
        source = zplus(offset) * NY + y
        for r in range(NY):
            spot = sel_ref[yplus(r), source]
            for kind in range(2):
                block = load(kind, spot)
                if r == 0:
                    fin_ref[source, kind] = block
                else:
                    stage[n, r - 1, kind] = block
        out = []
        for r in range(1, NY):
            out.append(
                copy(
                    stage.at[n, r - 1],
                    fin_ref.at[source],
                    scr["pick_s"].at[n, r - 1],
                    scr["pick_r"].at[n, r - 1],
                    at(z, yplus(r)),
                )
            )
        picks.extend(out)
        return out

    waiting = pick(0, 0, lambda kind, spot: (ck_ref, cv_ref)[kind][spot])

    hold = {}

    def row_totals():
        yall[y] = st_ref[y]
        for made in ya:
            made.wait_recv()
        for hh in range(2):
            rows = pl.ds(hh * HD, HD)
            total = jnp.zeros((1, HD), jnp.float32)
            state = jnp.zeros((HD, HD), jnp.float32)
            for k in range(NY):
                if k > 0:
                    pre[k, rows] = state
                    pre[k, pl.ds(2 * HD + hh, 1)] = total
                step = yall[k, pl.ds(2 * HD + hh, 1)]
                state = jnp.exp(step) * state + yall[k, rows]
                total = total + step
            tz[hh] = total
            rz[pl.ds(hh * 8, 8)] = state.astype(jnp.bfloat16).reshape(8, 16, HD)

    def send_totals():
        hold["za"] = []
        for r in range(1, NZ):
            to = zplus(r)
            one = copy(rz.at[to], zr.at[z], scr["za_s"].at[r - 1], scr["za_r"].at[r - 1], at(to, y))
            two = copy(
                tz.at[to // 8], zt.at[z], scr["zb_s"].at[r - 1], scr["zb_r"].at[r - 1], at(to, y)
            )
            one.start()
            two.start()
            hold["za"] += [one, two]
        zr[z] = rz[z]
        zt[z] = tz[z // 8]

    def scan():
        for made in hold["za"]:
            made.wait_recv()
        state = jnp.zeros((16, HD), jnp.float32)
        for k in range(NZ):
            ez[k] = state.astype(jnp.bfloat16)
            state = jnp.exp(zt[k]) * state + zr[k].astype(jnp.float32)

    def send_entering():
        hold["zc"] = []
        for r in range(1, NZ):
            to = zplus(r)
            one = copy(ez.at[to], er.at[z], scr["zc_s"].at[r - 1], scr["zc_r"].at[r - 1], at(to, y))
            one.start()
            hold["zc"].append(one)
        er[z] = ez[z]

    def members():
        for made in hold["zc"]:
            made.wait_recv()
        row = er[...].astype(jnp.float32).reshape(2 * HD, HD)
        eq[0] = row
        for k in range(1, NY):
            for hh in range(2):
                rows = pl.ds(hh * HD, HD)
                faded = jnp.exp(pre[k, pl.ds(2 * HD + hh, 1)]) * row[hh * HD : (hh + 1) * HD]
                eq[k, rows] = faded + pre[k, rows]

    def send_members():
        hold["yb"] = []
        for r in range(1, NY):
            to = yplus(r)
            one = copy(eq.at[to], ent_ref.at[y], scr["yb_s"].at[r - 1], scr["yb_r"].at[r - 1], at(z, to))
            one.start()
            hold["yb"].append(one)
        ent_ref[y] = eq[y]

    tasks = {
        (1, 0): row_totals,
        (1, 1): send_totals,
        (3, 1): scan,
        (3, 2): send_entering,
        (5, 1): members,
        (5, 2): send_members,
    }

    for d in range(1, NZ // 2 + 1):
        for c in range(4):
            for sign in (1, -1):
                if travels(sign, d, c):
                    ring[sign, d, c].wait_recv()
                if d < NZ // 2:
                    send_ring(sign, d + 1, c)
            if c == 0:
                for made in waiting:
                    made.start()
                waiting = []
            if (d, c) in tasks:
                tasks[d, c]()
        if d < NZ // 2:
            low, high = bufs_p[d - 1], bufs_m[d - 1]
            waiting = pick(2 * d - 1, NZ - d, lambda kind, spot, ref=low: ref[kind, spot])
            waiting += pick(2 * d, d, lambda kind, spot, ref=high: ref[kind, spot])
        else:
            waiting = pick(2 * d - 1, d, lambda kind, spot: far[kind, spot])
    for made in hold["yb"]:
        made.wait_recv()
    for made in waiting:
        made.start()
    for made in picks:
        made.wait_recv()
    for made in sends:
        made.wait_send()


def exchange(sel, ck, cv, st):
    names = {
        "bufs_p": [pltpu.VMEM((2, 8, BLOCK, HD), jnp.bfloat16)] * 7,
        "bufs_m": [pltpu.VMEM((2, 8, BLOCK, HD), jnp.bfloat16)] * 7,
        "far": pltpu.VMEM((2, 8, BLOCK, HD), jnp.bfloat16),
        "stage": pltpu.VMEM((NZ, NY - 1, 2, BLOCK, HD), jnp.bfloat16),
        "yall": pltpu.VMEM((NY, 264, HD), jnp.float32),
        "pre": pltpu.VMEM((NY, 264, HD), jnp.float32),
        "rz": pltpu.VMEM((NZ, 16, HD), jnp.bfloat16),
        "tz": pltpu.VMEM((2, 1, HD), jnp.float32),
        "zr": pltpu.VMEM((NZ, 16, HD), jnp.bfloat16),
        "zt": pltpu.VMEM((NZ, 1, HD), jnp.float32),
        "ez": pltpu.VMEM((NZ, 16, HD), jnp.bfloat16),
        "er": pltpu.VMEM((NZ, 16, HD), jnp.bfloat16),
        "eq": pltpu.VMEM((NY, 256, HD), jnp.float32),
        "ring_s": pltpu.SemaphoreType.DMA((2, 8, 4)),
        "ring_r": pltpu.SemaphoreType.DMA((2, 8, 4)),
        "pick_s": pltpu.SemaphoreType.DMA((NZ, NY - 1)),
        "pick_r": pltpu.SemaphoreType.DMA((NZ, NY - 1)),
        "ya_s": pltpu.SemaphoreType.DMA((NY - 1,)),
        "ya_r": pltpu.SemaphoreType.DMA((NY - 1,)),
        "yb_s": pltpu.SemaphoreType.DMA((NY - 1,)),
        "yb_r": pltpu.SemaphoreType.DMA((NY - 1,)),
        "za_s": pltpu.SemaphoreType.DMA((NZ - 1,)),
        "za_r": pltpu.SemaphoreType.DMA((NZ - 1,)),
        "zb_s": pltpu.SemaphoreType.DMA((NZ - 1,)),
        "zb_r": pltpu.SemaphoreType.DMA((NZ - 1,)),
        "zc_s": pltpu.SemaphoreType.DMA((NZ - 1,)),
        "zc_r": pltpu.SemaphoreType.DMA((NZ - 1,)),
    }
    flat, tree = jax.tree.flatten(names, is_leaf=lambda leaf: not isinstance(leaf, (dict, list)))

    def body(sel_ref, ck_ref, cv_ref, st_ref, fin_ref, ent_ref, *scratch):
        exchange_kernel(
            sel_ref, ck_ref, cv_ref, st_ref, fin_ref, ent_ref, jax.tree.unflatten(tree, scratch)
        )

    vmem = pl.BlockSpec(memory_space=pltpu.VMEM)
    return pl.pallas_call(
        body,
        out_shape=(
            jax.ShapeDtypeStruct((NZ * NY, 2, BLOCK, HD), jnp.bfloat16),
            jax.ShapeDtypeStruct((NY, 2 * HD, HD), jnp.float32),
        ),
        in_specs=[pl.BlockSpec(memory_space=pltpu.SMEM), vmem, vmem, vmem],
        out_specs=(vmem, vmem),
        scratch_shapes=flat,
        compiler_params=pltpu.CompilerParams(
            collective_id=0, has_side_effects=True, vmem_limit_bytes=VMEM_LIMIT
        ),
        name="exchange",
    )(sel, ck, cv, st)


NT = (((1,), (1,)), ((), ()))


def attend_kernel(src_ref, live_ref, q_ref, sk_ref, sv_ref, fin_ref, out_ref, qs, sc, top, tot, acc):
    factor = math.log2(math.e) / math.sqrt(HD)
    group = q_ref.shape[1] // HD
    rows = group * BLOCK
    chunk = 256

    for qb in range(2):
        tokens = pl.ds(qb * BLOCK, BLOCK)
        for g in range(group):
            qs[pl.ds(g * BLOCK, BLOCK)] = q_ref[tokens, g * HD : (g + 1) * HD]
        live = live_ref[qb]
        own = qb + 1

        def score(slot, keys, first=False, causal=False):
            for at in range(0, rows, chunk):
                part = pl.ds(at, chunk)
                s = lax.dot_general(qs[part], keys, NT, preferred_element_type=jnp.float32)
                if causal:
                    t = lax.broadcasted_iota(jnp.int32, (chunk, BLOCK), 0) % BLOCK
                    u = lax.broadcasted_iota(jnp.int32, (chunk, BLOCK), 1)
                    s = jnp.where(u <= t, s, -1e30)
                sc[slot, part] = s
                top[part] = s if first else jnp.maximum(top[part], s)

        score(0, sk_ref[tokens], first=True, causal=True)
        if qb == 1:
            score(1, sk_ref[pl.ds(0, BLOCK)])

        def more(j, carry):
            score(own + j, fin_ref[src_ref[qb, j], 0])
            return carry

        lax.fori_loop(0, live, more, 0)
        for at in range(0, rows, chunk):
            part = pl.ds(at, chunk)
            top[part] = jnp.broadcast_to(
                jnp.max(top[part], axis=1, keepdims=True) * factor, (chunk, BLOCK)
            )

        def mix(slot, values, first=False):
            for at in range(0, rows, chunk):
                part = pl.ds(at, chunk)
                w = jnp.exp2(sc[slot, part] * factor - top[part])
                m = jnp.dot(w.astype(jnp.bfloat16), values, preferred_element_type=jnp.float32)
                tot[part] = w if first else tot[part] + w
                acc[part] = m if first else acc[part] + m

        mix(0, sv_ref[tokens], first=True)
        if qb == 1:
            mix(1, sv_ref[pl.ds(0, BLOCK)])

        def again(j, carry):
            mix(own + j, fin_ref[src_ref[qb, j], 1])
            return carry

        lax.fori_loop(0, live, again, 0)
        for g in range(group):
            part = pl.ds(g * BLOCK, BLOCK)
            whole = jnp.sum(tot[part], axis=1, keepdims=True)
            out_ref[tokens, g * HD : (g + 1) * HD] = (acc[part] / whole).astype(jnp.bfloat16)


def attend(sources, live, queries, keys, values, fin):
    tok_rows, width = queries.shape
    rows = width // HD * BLOCK
    vmem = pl.BlockSpec(memory_space=pltpu.VMEM)
    smem = pl.BlockSpec(memory_space=pltpu.SMEM)
    return pl.pallas_call(
        attend_kernel,
        out_shape=jax.ShapeDtypeStruct((tok_rows, width), jnp.bfloat16),
        in_specs=[smem, smem, vmem, vmem, vmem, vmem],
        out_specs=vmem,
        scratch_shapes=[
            pltpu.VMEM((rows, HD), jnp.bfloat16),
            pltpu.VMEM((18, rows, BLOCK), jnp.float32),
            pltpu.VMEM((rows, BLOCK), jnp.float32),
            pltpu.VMEM((rows, BLOCK), jnp.float32),
            pltpu.VMEM((rows, HD), jnp.float32),
        ],
        compiler_params=pltpu.CompilerParams(vmem_limit_bytes=VMEM_LIMIT),
        name="attend",
    )(sources, live, queries, keys, values, fin)


def tables(block_lists, live_counts):
    place = lax.axis_index("ctx")
    selected = block_lists.shape[1]
    row = place // NY
    lists = lax.dynamic_slice_in_dim(block_lists, row * 2 * NY, 2 * NY, 0)
    counts = lax.dynamic_slice_in_dim(live_counts, row * 2 * NY, 2 * NY, 0)
    read = jnp.arange(selected, dtype=jnp.int32)[None, :] < counts[:, None]
    flat = jnp.where(read, lists, -1).reshape(NY, 2 * selected)
    owners = jnp.arange(NZ * NY, dtype=jnp.int32)
    hit = (flat >> 3)[:, :, None] == owners[None, None, :]
    sel = jnp.max(jnp.where(hit, (flat & 7)[:, :, None], 0), axis=1)
    mine = lax.dynamic_slice_in_dim(block_lists, place * 2, 2, 0) >> 3
    my_counts = lax.dynamic_slice_in_dim(live_counts, place * 2, 2, 0)
    return sel, mine, my_counts


def local(
    lin_queries,
    lin_keys,
    lin_values,
    log_decay,
    lin_gate,
    norm_gain,
    soft_queries,
    slab_keys,
    slab_values,
    cache_keys,
    cache_values,
    block_lists,
    live_counts,
):
    tok_rows = lin_queries.shape[0]
    head_count = lin_queries.shape[1] // HD
    sel, mine, my_counts = tables(block_lists, live_counts)
    act_queries = (
        jax.nn.silu(lin_queries.astype(jnp.float32))
        .astype(jnp.bfloat16)
        .reshape(tok_rows, head_count, HD)
    )
    act_keys = (
        jax.nn.silu(lin_keys.astype(jnp.float32))
        .astype(jnp.bfloat16)
        .reshape(tok_rows, head_count, HD)
    )
    values_here = lin_values.reshape(tok_rows, head_count, HD)
    running = jnp.cumsum(log_decay, axis=0)
    seg_total = running[-1]
    fade = jnp.exp(seg_total[None, :] - running)
    seg_state = jnp.einsum(
        "shd,she->hde",
        act_keys.astype(jnp.float32) * fade[:, :, None],
        values_here.astype(jnp.float32),
        precision=lax.Precision.HIGHEST,
    )
    st = jnp.concatenate(
        [
            seg_state.reshape(NY, 2 * HD, HD),
            jnp.broadcast_to(seg_total.reshape(NY, 2)[:, :, None], (NY, 2, HD)),
            jnp.zeros((NY, 6, HD), jnp.float32),
        ],
        axis=1,
    )
    blocks = cache_keys.shape[0] // BLOCK
    fin, entering = exchange(
        sel,
        cache_keys.reshape(blocks, BLOCK, HD),
        cache_values.reshape(blocks, BLOCK, HD),
        st,
    )
    entering = entering.reshape(head_count, HD, HD)
    soft_out = attend(mine, my_counts, soft_queries, slab_keys, slab_values, fin)

    flipped = running.T
    gaps = flipped[:, :, None] - flipped[:, None, :]
    causal = jnp.arange(tok_rows)[:, None] >= jnp.arange(tok_rows)[None, :]
    weight = jnp.where(causal[None], jnp.exp(jnp.minimum(gaps, 0.0)), 0.0)
    scores = jnp.einsum("thd,shd->hts", act_queries, act_keys, preferred_element_type=jnp.float32)
    lin_scores = (scores * weight).astype(jnp.bfloat16)
    intra = jnp.einsum("hts,shd->thd", lin_scores, values_here, preferred_element_type=jnp.float32)
    inter = jnp.exp(running)[:, :, None] * jnp.einsum(
        "thd,hde->the", act_queries.astype(jnp.float32), entering, precision=lax.Precision.HIGHEST
    )
    lin_attn = (intra + inter).reshape(tok_rows, head_count * HD)
    partial_squares = jnp.sum(lin_attn * lin_attn, axis=1)
    whole_squares = lax.psum(partial_squares, "head")
    scaling = lax.rsqrt(whole_squares / (QUERY_HEADS * HD) + 1e-06)
    gated = (
        lin_attn
        * scaling[:, None]
        * norm_gain[None, :]
        * jax.nn.sigmoid(lin_gate.astype(jnp.float32))
    )
    return (gated.astype(jnp.bfloat16), soft_out)


def solution(mesh):
    in_specs = (
        P("ctx", "head"),
        P("ctx", "head"),
        P("ctx", "head"),
        P("ctx", "head"),
        P("ctx", "head"),
        P("head"),
        P("ctx", "head"),
        P("ctx", "head"),
        P("ctx", "head"),
        P("ctx", "head"),
        P("ctx", "head"),
        P(),
        P(),
    )
    out_specs = (P("ctx", "head"), P("ctx", "head"))
    return jax.shard_map(local, mesh=mesh, in_specs=in_specs, out_specs=out_specs, check_vma=False)
```

```python
import functools
import math

import jax
import jax.numpy as jnp
from jax import lax
from jax.experimental import pallas as pl
from jax.experimental.pallas import tpu as pltpu
from jax.sharding import PartitionSpec as P

QUERY_HEADS = 64
HD = 128
BLOCK = 128
NZ = 16
NY = 4
MESH = pl.DeviceIdType.MESH
VMEM_LIMIT = 60 * 1024 * 1024


NT = (((1,), (1,)), ((), ()))
TN = (((0,), (0,)), ((), ()))
LAST = 6
HIGHEST = lax.Precision.HIGHEST


def exchange_kernel(
    sel_ref, ck_ref, cv_ref, lq_ref, lk_ref, lv_ref, lg_ref, ld_ref, gain_ref, fin_ref, lin_ref, scr
):
    me = lax.axis_index("ctx")
    mine = lax.axis_index("head")
    z = me // NY
    y = me % NY
    heads = 2 * NY

    def zplus(k):
        return (z + k) % NZ

    def yplus(k):
        return (y + k) % NY

    def at(zz, yy):
        return {"ctx": zz * NY + yy, "head": mine}

    def beside(r):
        return {"ctx": me, "head": (mine + r) % heads}

    sends = []

    def copy(src, dst, ssem, rsem, where):
        made = pltpu.make_async_remote_copy(
            src_ref=src,
            dst_ref=dst,
            send_sem=ssem,
            recv_sem=rsem,
            device_id=where,
            device_id_type=MESH,
        )
        sends.append(made)
        return made

    lq, lk, lv, lg, own_k, own_v = (scr[n] for n in ("lq", "lk", "lv", "lg", "own_k", "own_v"))
    loads = {}
    for n, (name, src, dst) in enumerate(
        (
            ("k", lk_ref, lk),
            ("v", lv_ref, lv),
            ("ck", ck_ref, own_k),
            ("cv", cv_ref, own_v),
            ("q", lq_ref, lq),
            ("g", lg_ref, lg),
        )
    ):
        loads[name] = pltpu.make_async_copy(src, dst, scr["in_s"].at[n])
        loads[name].start()

    barrier = pltpu.get_barrier_semaphore()
    friends = [at(z, yplus(r)) for r in range(1, NY)]
    friends += [at(zplus(r), y) for r in range(1, NZ)]
    friends += [at(zplus(k), yplus(r)) for k in (1, 2, NZ - 1, NZ - 2) for r in range(1, NY)]
    friends += [beside(r) for r in range(1, heads)]
    for friend in friends:
        pl.semaphore_signal(barrier, inc=1, device_id=friend, device_id_type=MESH)
    pl.semaphore_wait(barrier, len(friends))

    bufs = {
        (sign, d): scr["bufs"][2 * (2 * (d - 1) + (sign < 0)) :][:2]
        for d in range(1, LAST + 1)
        for sign in (1, -1)
    }
    ring = {}

    def send_ring(sign, d, c):
        half = pl.ds(4 * (c % 2), 4)
        src = (ck_ref, cv_ref)[c // 2] if d == 1 else bufs[sign, d - 1][c // 2]
        k = 0 if sign > 0 else 1
        made = copy(
            src.at[half],
            bufs[sign, d][c // 2].at[half],
            scr["ring_s"].at[k, d - 1, c],
            scr["ring_r"].at[k, d - 1, c],
            at(zplus(1 if sign > 0 else NZ - 1), y),
        )
        ring[sign, d, c] = made
        made.start()

    for c in range(4):
        send_ring(1, 1, c)
        send_ring(-1, 1, c)

    decay = ld_ref[...]
    tokens = decay.shape[0]
    row_id = lax.broadcasted_iota(jnp.int32, (tokens, tokens), 0)
    col_id = lax.broadcasted_iota(jnp.int32, (tokens, tokens), 1)
    triangle = jnp.where(col_id <= row_id, 1.0, 0.0).astype(jnp.float32)
    down_all = scr["down"]
    down_all[...] = lax.dot_general(
        triangle, decay, (((1,), (0,)), ((), ())), precision=HIGHEST, preferred_element_type=jnp.float32
    )
    across_all = scr["across"]
    across_all[...] = lax.dot_general(
        decay, triangle, (((0,), (1,)), ((), ())), precision=HIGHEST, preferred_element_type=jnp.float32
    )

    def silu(u):
        return u / (1.0 + jnp.exp(-u))

    def lanes(h):
        return slice(h * HD, (h + 1) * HD)

    st = scr["st"]
    loads["k"].wait()
    loads["v"].wait()
    for h in range(heads):
        down = down_all[:, h : h + 1]
        total = down[tokens - 1 : tokens]
        key = silu(lk[:, lanes(h)].astype(jnp.float32)).astype(jnp.bfloat16)
        lk[:, lanes(h)] = key
        faded = key.astype(jnp.float32) * jnp.exp(total - down)
        high = faded.astype(jnp.bfloat16)
        low = (faded - high.astype(jnp.float32)).astype(jnp.bfloat16)
        value = lv[:, lanes(h)]
        state = lax.dot_general(high, value, TN, preferred_element_type=jnp.float32)
        state += lax.dot_general(low, value, TN, preferred_element_type=jnp.float32)
        st[h // 2, pl.ds((h % 2) * HD, HD)] = state
        st[h // 2, pl.ds(2 * HD + h % 2, 1)] = jnp.broadcast_to(total, (1, HD))

    yall, rz, tz, zr, zt = scr["yall"], scr["rz"], scr["tz"], scr["zr"], scr["zt"]
    ez, er, eq, pre, ent = scr["ez"], scr["er"], scr["eq"], scr["pre"], scr["ent"]

    stage, far = scr["stage"], scr["far"]
    picks = []

    def pick(n, offset, refs, kinds):
        source = zplus(offset) * NY + y
        for r in range(NY):
            spot = sel_ref[z * NY + yplus(r), source]
            for kind in kinds:
                block = refs[kind][spot]
                if r == 0:
                    fin_ref[source, kind] = block
                else:
                    stage[n, r - 1, kind] = block
        out = []
        for r in range(1, NY):
            for kind in kinds if len(kinds) == 1 else (None,):
                a, b, c = stage.at[n, r - 1], fin_ref.at[source], 0
                if kind is not None:
                    a, b, c = a.at[kind], b.at[kind], kind
                out.append(
                    copy(
                        a,
                        b,
                        scr["pick_s"].at[n, r - 1, c],
                        scr["pick_r"].at[n, r - 1, c],
                        at(z, yplus(r)),
                    )
                )
        picks.extend(out)
        return out

    def pick_far(sign, kind):
        k = 0 if sign > 0 else 1
        source = zplus(NZ - LAST * sign) * NY + y
        out = []
        for beyond in (1, 2):
            to = zplus(NZ + sign * beyond)
            for r in range(NY):
                if beyond == 2 and (r < 2) != (sign > 0):
                    continue
                spot = sel_ref[to * NY + yplus(r), source]
                far[k, beyond - 1, r, kind] = bufs[sign, LAST][kind][spot]
                out.append(
                    copy(
                        far.at[k, beyond - 1, r, kind],
                        fin_ref.at[source, kind],
                        scr["far_s"].at[k, beyond - 1, r, kind],
                        scr["far_r"].at[k, beyond - 1, r, kind],
                        at(to, yplus(r)),
                    )
                )
        picks.extend(out)
        return out

    hold = {}

    def send_states():
        hold["ya"] = []
        for r in range(1, NY):
            made = copy(
                st.at[yplus(r)],
                yall.at[y],
                scr["ya_s"].at[r - 1],
                scr["ya_r"].at[r - 1],
                at(z, yplus(r)),
            )
            made.start()
            hold["ya"].append(made)

    def row_totals():
        yall[y] = st[y]
        for made in hold["ya"]:
            made.wait_recv()
        for hh in range(2):
            rows = pl.ds(hh * HD, HD)
            total = jnp.zeros((1, HD), jnp.float32)
            state = jnp.zeros((HD, HD), jnp.float32)
            for k in range(NY):
                if k > 0:
                    pre[k, rows] = state
                    pre[k, pl.ds(2 * HD + hh, 1)] = total
                step = yall[k, pl.ds(2 * HD + hh, 1)]
                state = jnp.exp(step) * state + yall[k, rows]
                total = total + step
            tz[hh] = total
            rz[pl.ds(hh * 8, 8)] = state.astype(jnp.bfloat16).reshape(8, 16, HD)

    def send_totals():
        hold["za"] = []
        for r in range(1, NZ):
            to = zplus(r)
            one = copy(rz.at[to], zr.at[z], scr["za_s"].at[r - 1], scr["za_r"].at[r - 1], at(to, y))
            two = copy(
                tz.at[to // 8], zt.at[z], scr["zb_s"].at[r - 1], scr["zb_r"].at[r - 1], at(to, y)
            )
            one.start()
            two.start()
            hold["za"] += [one, two]
        zr[z] = rz[z]
        zt[z] = tz[z // 8]

    def scan():
        for made in hold["za"]:
            made.wait_recv()
        state = jnp.zeros((16, HD), jnp.float32)
        for k in range(NZ):
            ez[k] = state.astype(jnp.bfloat16)
            state = jnp.exp(zt[k]) * state + zr[k].astype(jnp.float32)

    def send_entering():
        hold["zc"] = []
        for r in range(1, NZ):
            to = zplus(r)
            one = copy(ez.at[to], er.at[z], scr["zc_s"].at[r - 1], scr["zc_r"].at[r - 1], at(to, y))
            one.start()
            hold["zc"].append(one)
        er[z] = ez[z]

    def members():
        for made in hold["zc"]:
            made.wait_recv()
        row = er[...].astype(jnp.float32).reshape(2 * HD, HD)
        eq[0] = row
        for k in range(1, NY):
            for hh in range(2):
                rows = pl.ds(hh * HD, HD)
                faded = jnp.exp(pre[k, pl.ds(2 * HD + hh, 1)]) * row[hh * HD : (hh + 1) * HD]
                eq[k, rows] = faded + pre[k, rows]

    def send_members():
        hold["yb"] = []
        for r in range(1, NY):
            to = yplus(r)
            one = copy(eq.at[to], ent.at[y], scr["yb_s"].at[r - 1], scr["yb_r"].at[r - 1], at(z, to))
            one.start()
            hold["yb"].append(one)
        ent[y] = eq[y]

    attn = scr["attn"]

    def intra(h):
        if h == 0:
            loads["q"].wait()
        query = silu(lq[:, lanes(h)].astype(jnp.float32)).astype(jnp.bfloat16)
        lq[:, lanes(h)] = query
        scores = lax.dot_general(query, lk[:, lanes(h)], NT, preferred_element_type=jnp.float32)
        gaps = down_all[:, h : h + 1] - across_all[h : h + 1, :]
        t = lax.broadcasted_iota(jnp.int32, (tokens, tokens), 0)
        u = lax.broadcasted_iota(jnp.int32, (tokens, tokens), 1)
        weight = jnp.where(u <= t, jnp.exp(jnp.minimum(gaps, 0.0)), 0.0)
        attn[:, lanes(h)] = jnp.dot(
            (scores * weight).astype(jnp.bfloat16), lv[:, lanes(h)], preferred_element_type=jnp.float32
        )

    squares, norms = scr["squares"], scr["norms"]

    def inter(h):
        state = ent[h // 2, pl.ds((h % 2) * HD, HD)]
        high = state.astype(jnp.bfloat16)
        low = (state - high.astype(jnp.float32)).astype(jnp.bfloat16)
        query = lq[:, lanes(h)]
        moved = jnp.dot(query, high, preferred_element_type=jnp.float32)
        moved += jnp.dot(query, low, preferred_element_type=jnp.float32)
        whole = attn[:, lanes(h)] + jnp.exp(down_all[:, h : h + 1]) * moved
        attn[:, lanes(h)] = whole
        squares[...] = whole * whole if h == 0 else squares[...] + whole * whole

    def send_squares():
        norms[0] = lax.dot_general(
            jnp.ones((8, HD), jnp.float32),
            squares[...],
            NT,
            precision=HIGHEST,
            preferred_element_type=jnp.float32,
        )

    def start_squares():
        hold["sq"] = []
        for r in range(1, heads):
            one = copy(
                norms.at[0], norms.at[r], scr["sq_s"].at[r - 1], scr["sq_r"].at[r - 1], beside(r)
            )
            one.start()
            hold["sq"].append(one)

    def gate():
        for made in hold["sq"]:
            made.wait_recv()
        summed = norms[0]
        for r in range(1, heads):
            summed = summed + norms[r]
        first = jnp.where(lax.broadcasted_iota(jnp.int32, (8, HD), 0) == 0, 1.0, 0.0)
        tall = lax.dot_general(
            summed,
            first.astype(jnp.float32),
            TN,
            precision=HIGHEST,
            preferred_element_type=jnp.float32,
        )
        scaling = lax.rsqrt(tall / (QUERY_HEADS * HD) + 1e-06)
        loads["g"].wait()
        for h in range(heads):
            opened = 1.0 + jnp.exp(-lg[:, lanes(h)].astype(jnp.float32))
            shaped = attn[:, lanes(h)] * scaling * gain_ref[:, lanes(h)]
            lin_ref[:, lanes(h)] = (shaped / opened).astype(jnp.bfloat16)

    loads["ck"].wait()
    loads["cv"].wait()
    send_states()
    waiting = pick(0, 0, (own_k, own_v), (0, 1))
    tasks = {
        (1, 2): [row_totals],
        (1, 3): [send_totals],
        (2, 0): [lambda: intra(0)],
        (2, 1): [lambda: intra(1)],
        (2, 2): [lambda: intra(2)],
        (2, 3): [lambda: intra(3)],
        (3, 1): [scan],
        (3, 2): [send_entering],
        (4, 0): [lambda: intra(4)],
        (4, 1): [lambda: intra(5)],
        (4, 2): [lambda: intra(6)],
        (4, 3): [lambda: intra(7)],
        (5, 1): [members],
        (5, 2): [send_members],
    }
    for d in range(1, LAST + 1):
        for c in range(4):
            for sign in (1, -1):
                ring[sign, d, c].wait_recv()
                if d < LAST:
                    send_ring(sign, d + 1, c)
            for made in waiting:
                made.start()
            waiting = []
            for task in tasks.get((d, c), []):
                task()
            if d == LAST and c % 2 == 1:
                kind = c // 2
                waiting = pick_far(1, kind) + pick_far(-1, kind)
                waiting += pick(2 * d - 1, NZ - d, bufs[1, d], (kind,))
                waiting += pick(2 * d, d, bufs[-1, d], (kind,))
        if d < LAST:
            waiting = pick(2 * d - 1, NZ - d, bufs[1, d], (0, 1))
            waiting += pick(2 * d, d, bufs[-1, d], (0, 1))
    for made in waiting:
        made.start()
    for made in hold["yb"]:
        made.wait_recv()
    for h in range(heads):
        inter(h)
    send_squares()
    start_squares()
    gate()
    for made in picks:
        made.wait_recv()
    for made in sends:
        made.wait_send()


def exchange(sel, ck, cv, lq, lk, lv, lg, ld, gain):
    tokens, width = lq.shape
    shards = 2 * LAST + 1
    dma = pltpu.SemaphoreType.DMA
    names = {
        "bufs": [pltpu.VMEM((8, BLOCK, HD), jnp.bfloat16)] * (4 * LAST),
        "own_k": pltpu.VMEM((8, BLOCK, HD), jnp.bfloat16),
        "own_v": pltpu.VMEM((8, BLOCK, HD), jnp.bfloat16),
        "stage": pltpu.VMEM((shards, NY - 1, 2, BLOCK, HD), jnp.bfloat16),
        "far": pltpu.VMEM((2, 2, NY, 2, BLOCK, HD), jnp.bfloat16),
        "lq": pltpu.VMEM((tokens, width), jnp.bfloat16),
        "lk": pltpu.VMEM((tokens, width), jnp.bfloat16),
        "lv": pltpu.VMEM((tokens, width), jnp.bfloat16),
        "lg": pltpu.VMEM((tokens, width), jnp.bfloat16),
        "attn": pltpu.VMEM((tokens, width), jnp.float32),
        "squares": pltpu.VMEM((tokens, HD), jnp.float32),
        "norms": pltpu.VMEM((8, 8, tokens), jnp.float32),
        "down": pltpu.VMEM((tokens, 8), jnp.float32),
        "across": pltpu.VMEM((8, tokens), jnp.float32),
        "st": pltpu.VMEM((NY, 264, HD), jnp.float32),
        "yall": pltpu.VMEM((NY, 264, HD), jnp.float32),
        "pre": pltpu.VMEM((NY, 264, HD), jnp.float32),
        "rz": pltpu.VMEM((NZ, 16, HD), jnp.bfloat16),
        "tz": pltpu.VMEM((2, 1, HD), jnp.float32),
        "zr": pltpu.VMEM((NZ, 16, HD), jnp.bfloat16),
        "zt": pltpu.VMEM((NZ, 1, HD), jnp.float32),
        "ez": pltpu.VMEM((NZ, 16, HD), jnp.bfloat16),
        "er": pltpu.VMEM((NZ, 16, HD), jnp.bfloat16),
        "eq": pltpu.VMEM((NY, 256, HD), jnp.float32),
        "ent": pltpu.VMEM((NY, 256, HD), jnp.float32),
        "in_s": dma((6,)),
        "ring_s": dma((2, LAST, 4)),
        "ring_r": dma((2, LAST, 4)),
        "pick_s": dma((shards, NY - 1, 2)),
        "pick_r": dma((shards, NY - 1, 2)),
        "far_s": dma((2, 2, NY, 2)),
        "far_r": dma((2, 2, NY, 2)),
        "ya_s": dma((NY - 1,)),
        "ya_r": dma((NY - 1,)),
        "yb_s": dma((NY - 1,)),
        "yb_r": dma((NY - 1,)),
        "za_s": dma((NZ - 1,)),
        "za_r": dma((NZ - 1,)),
        "zb_s": dma((NZ - 1,)),
        "zb_r": dma((NZ - 1,)),
        "zc_s": dma((NZ - 1,)),
        "zc_r": dma((NZ - 1,)),
        "sq_s": dma((7,)),
        "sq_r": dma((7,)),
    }
    flat, tree = jax.tree.flatten(names, is_leaf=lambda leaf: not isinstance(leaf, (dict, list)))

    def body(*refs):
        exchange_kernel(*refs[:11], jax.tree.unflatten(tree, refs[11:]))

    vmem = pl.BlockSpec(memory_space=pltpu.VMEM)
    hbm = pl.BlockSpec(memory_space=pl.ANY)
    return pl.pallas_call(
        body,
        out_shape=(
            jax.ShapeDtypeStruct((NZ * NY, 2, BLOCK, HD), jnp.bfloat16),
            jax.ShapeDtypeStruct((tokens, width), jnp.bfloat16),
        ),
        in_specs=[pl.BlockSpec(memory_space=pltpu.SMEM)] + [hbm] * 6 + [vmem] * 2,
        out_specs=(vmem, vmem),
        scratch_shapes=flat,
        compiler_params=pltpu.CompilerParams(
            collective_id=0, has_side_effects=True, vmem_limit_bytes=VMEM_LIMIT
        ),
        name="exchange",
    )(sel, ck, cv, lq, lk, lv, lg, ld, gain)


GROUP = 4


def attend_kernel(lists_ref, counts_ref, q_ref, sk_ref, sv_ref, fin_ref, out_ref, qs, keys, values, sc, top, tot, acc):
    me = lax.axis_index("ctx")
    factor = math.log2(math.e) / math.sqrt(HD)
    heads = q_ref.shape[1] // HD
    selected = lists_ref.shape[1]
    rows = heads * BLOCK
    chunk = BLOCK
    wide = GROUP * BLOCK

    def parts(full):
        return [full[:, i * BLOCK : (i + 1) * BLOCK] for i in range(GROUP)]

    for qb in range(2):
        tokens = pl.ds(qb * BLOCK, BLOCK)
        query_block = 2 * me + qb
        own = qb + 1
        for g in range(heads):
            qs[pl.ds(g * BLOCK, BLOCK)] = q_ref[tokens, g * HD : (g + 1) * HD]
        keys[0:BLOCK] = sk_ref[tokens]
        values[0:BLOCK] = sv_ref[tokens]
        if qb == 1:
            keys[BLOCK : 2 * BLOCK] = sk_ref[0:BLOCK]
            values[BLOCK : 2 * BLOCK] = sv_ref[0:BLOCK]
        for j in range(selected):
            source = lists_ref[query_block, j] >> 3
            place = pl.ds((own + j) * BLOCK, BLOCK)
            keys[place] = fin_ref[source, 0]
            values[place] = fin_ref[source, 1]
        if own + selected < 5 * GROUP:
            place = pl.ds((own + selected) * BLOCK, (5 * GROUP - own - selected) * BLOCK)
            keys[place] = jnp.zeros(((5 * GROUP - own - selected) * BLOCK, HD), jnp.bfloat16)
            values[place] = jnp.zeros(((5 * GROUP - own - selected) * BLOCK, HD), jnp.bfloat16)
        filled = (own + counts_ref[query_block]) * BLOCK

        def score(n, first):
            base = 0 if first else pl.multiple_of(n * wide, wide)
            these = keys[pl.ds(base, wide)]
            for at in range(0, rows, chunk):
                part = pl.ds(at, chunk)
                s = lax.dot_general(qs[part], these, NT, preferred_element_type=jnp.float32)
                u = lax.broadcasted_iota(jnp.int32, (chunk, wide), 1)
                keep = u < filled - base
                if first:
                    t = lax.broadcasted_iota(jnp.int32, (chunk, wide), 0)
                    keep = keep & ((u <= t) | (u >= BLOCK))
                s = jnp.where(keep, s, -1e30)
                sc[n, part] = s
                most = functools.reduce(jnp.maximum, parts(s))
                top[part] = most if first else jnp.maximum(top[part], most)

        def mix(n, first):
            base = 0 if first else pl.multiple_of(n * wide, wide)
            these = values[pl.ds(base, wide)]
            for at in range(0, rows, chunk):
                part = pl.ds(at, chunk)
                peak = top[part]
                w = [jnp.exp2(s * factor - peak) for s in parts(sc[n, part])]
                m = jnp.dot(
                    jnp.concatenate([piece.astype(jnp.bfloat16) for piece in w], axis=1),
                    these,
                    preferred_element_type=jnp.float32,
                )
                some = functools.reduce(jnp.add, w)
                tot[part] = some if first else tot[part] + some
                acc[part] = m if first else acc[part] + m

        def body(step):
            def run(n, carry):
                step(n, False)
                return carry

            return run

        groups = (filled + wide - 1) // wide
        score(0, True)
        lax.fori_loop(1, groups, body(score), 0)
        for at in range(0, rows, chunk):
            part = pl.ds(at, chunk)
            top[part] = jnp.broadcast_to(
                jnp.max(top[part], axis=1, keepdims=True) * factor, (chunk, BLOCK)
            )
        mix(0, True)
        lax.fori_loop(1, groups, body(mix), 0)
        for g in range(heads):
            part = pl.ds(g * BLOCK, BLOCK)
            whole = jnp.sum(tot[part], axis=1, keepdims=True)
            out_ref[tokens, g * HD : (g + 1) * HD] = (acc[part] / whole).astype(jnp.bfloat16)


def attend(lists, counts, queries, keys, values, fin):
    tok_rows, width = queries.shape
    rows = width // HD * BLOCK
    vmem = pl.BlockSpec(memory_space=pltpu.VMEM)
    smem = pl.BlockSpec(memory_space=pltpu.SMEM)
    return pl.pallas_call(
        attend_kernel,
        out_shape=jax.ShapeDtypeStruct((tok_rows, width), jnp.bfloat16),
        in_specs=[smem, smem, vmem, vmem, vmem, vmem],
        out_specs=vmem,
        scratch_shapes=[
            pltpu.VMEM((rows, HD), jnp.bfloat16),
            pltpu.VMEM((5 * GROUP * BLOCK, HD), jnp.bfloat16),
            pltpu.VMEM((5 * GROUP * BLOCK, HD), jnp.bfloat16),
            pltpu.VMEM((5, rows, GROUP * BLOCK), jnp.float32),
            pltpu.VMEM((rows, BLOCK), jnp.float32),
            pltpu.VMEM((rows, BLOCK), jnp.float32),
            pltpu.VMEM((rows, HD), jnp.float32),
        ],
        compiler_params=pltpu.CompilerParams(vmem_limit_bytes=VMEM_LIMIT),
        name="attend",
    )(lists, counts, queries, keys, values, fin)


def table(block_lists, live_counts):
    selected = block_lists.shape[1]
    read = jnp.arange(selected, dtype=jnp.int32)[None, :] < live_counts[:, None]
    flat = jnp.where(read, block_lists, -1).reshape(NZ * NY, 2 * selected)
    owners = jnp.arange(NZ * NY, dtype=jnp.int32)
    hit = (flat >> 3)[:, :, None] == owners[None, None, :]
    return jnp.max(jnp.where(hit, (flat & 7)[:, :, None], 0), axis=1)


def local(
    lin_queries,
    lin_keys,
    lin_values,
    log_decay,
    lin_gate,
    norm_gain,
    soft_queries,
    slab_keys,
    slab_values,
    cache_keys,
    cache_values,
    block_lists,
    live_counts,
):
    blocks = cache_keys.shape[0] // BLOCK
    fin, lin_out = exchange(
        table(block_lists, live_counts),
        cache_keys.reshape(blocks, BLOCK, HD),
        cache_values.reshape(blocks, BLOCK, HD),
        lin_queries,
        lin_keys,
        lin_values,
        lin_gate,
        log_decay,
        norm_gain.reshape(1, -1),
    )
    soft_out = attend(block_lists, live_counts, soft_queries, slab_keys, slab_values, fin)
    return (lin_out, soft_out)


def solution(mesh):
    in_specs = (
        P("ctx", "head"),
        P("ctx", "head"),
        P("ctx", "head"),
        P("ctx", "head"),
        P("ctx", "head"),
        P("head"),
        P("ctx", "head"),
        P("ctx", "head"),
        P("ctx", "head"),
        P("ctx", "head"),
        P("ctx", "head"),
        P(),
        P(),
    )
    out_specs = (P("ctx", "head"), P("ctx", "head"))
    return jax.shard_map(local, mesh=mesh, in_specs=in_specs, out_specs=out_specs, check_vma=False)
```

```python
import functools
import math

import jax
import jax.numpy as jnp
from jax import lax
from jax.experimental import pallas as pl
from jax.experimental.pallas import tpu as pltpu
from jax.sharding import PartitionSpec as P

QUERY_HEADS = 64
HD = 128
BLOCK = 128
NZ = 16
NY = 4
MESH = pl.DeviceIdType.MESH
VMEM_LIMIT = 60 * 1024 * 1024


NT = (((1,), (1,)), ((), ()))
TN = (((0,), (0,)), ((), ()))
LAST = 6
CHUNKS = 4
PER = 16 // CHUNKS
HIGHEST = lax.Precision.HIGHEST


def exchange_kernel(
    sel_ref, ck_ref, cv_ref, lq_ref, lk_ref, lv_ref, lg_ref, ld_ref, gain_ref, fin_ref, lin_ref, scr
):
    me = lax.axis_index("ctx")
    mine = lax.axis_index("head")
    z = me // NY
    y = me % NY
    heads = 2 * NY

    def zplus(k):
        return (z + k) % NZ

    def yplus(k):
        return (y + k) % NY

    def at(zz, yy):
        return {"ctx": zz * NY + yy, "head": mine}

    def beside(r):
        return {"ctx": me, "head": (mine + r) % heads}

    sends = []

    def copy(src, dst, ssem, rsem, where):
        made = pltpu.make_async_remote_copy(
            src_ref=src,
            dst_ref=dst,
            send_sem=ssem,
            recv_sem=rsem,
            device_id=where,
            device_id_type=MESH,
        )
        sends.append(made)
        return made

    lq, lk, lv, lg, own_k, own_v = (scr[n] for n in ("lq", "lk", "lv", "lg", "own_k", "own_v"))
    loads = {}
    for n, (name, src, dst) in enumerate(
        (
            ("k", lk_ref, lk),
            ("v", lv_ref, lv),
            ("ck", ck_ref, own_k),
            ("cv", cv_ref, own_v),
            ("q", lq_ref, lq),
            ("g", lg_ref, lg),
        )
    ):
        loads[name] = pltpu.make_async_copy(src, dst, scr["in_s"].at[n])
        loads[name].start()

    barrier = pltpu.get_barrier_semaphore()
    friends = [at(z, yplus(r)) for r in range(1, NY)]
    friends += [at(zplus(1), y), at(zplus(NZ - 1), y)]
    friends += [beside(r) for r in range(1, heads)]
    for friend in friends:
        pl.semaphore_signal(barrier, inc=1, device_id=friend, device_id_type=MESH)
    pl.semaphore_wait(barrier, len(friends))

    bufs = {
        (sign, d): scr["bufs"][2 * (2 * (d - 1) + (sign < 0)) :][:2]
        for d in range(1, LAST + 1)
        for sign in (1, -1)
    }
    ring = {}

    def send_ring(sign, d, c):
        kind = c * 2 // CHUNKS
        half = pl.ds(PER * c % 8, PER)
        src = (ck_ref, cv_ref)[kind] if d == 1 else bufs[sign, d - 1][kind]
        k = 0 if sign > 0 else 1
        made = copy(
            src.at[half],
            bufs[sign, d][kind].at[half],
            scr["ring_s"].at[k, d - 1, c],
            scr["ring_r"].at[k, d - 1, c],
            at(zplus(1 if sign > 0 else NZ - 1), y),
        )
        ring[sign, d, c] = made
        made.start()

    for c in range(CHUNKS):
        send_ring(1, 1, c)
        send_ring(-1, 1, c)

    def spread():
        for k in range(NZ // 2):
            for n, to in enumerate((zplus(1), zplus(NZ - 1))):
                pl.semaphore_signal(
                    scr["near"].at[n], inc=1, device_id=at(to, y), device_id_type=MESH
                )
            for n in range(2):
                pl.semaphore_wait(scr["near"].at[n], 1)

    decay = ld_ref[...]
    tokens = decay.shape[1]
    row_id = lax.broadcasted_iota(jnp.int32, (tokens, tokens), 0)
    col_id = lax.broadcasted_iota(jnp.int32, (tokens, tokens), 1)
    triangle = jnp.where(col_id <= row_id, 1.0, 0.0).astype(jnp.float32)
    down_all = scr["down"]
    down_all[...] = lax.dot_general(
        triangle, decay, NT, precision=HIGHEST, preferred_element_type=jnp.float32
    )
    across_all = scr["across"]
    across_all[...] = lax.dot_general(
        decay, triangle, NT, precision=HIGHEST, preferred_element_type=jnp.float32
    )

    def silu(u):
        return u / (1.0 + jnp.exp(-u))

    def lanes(h):
        return slice(h * HD, (h + 1) * HD)

    st = scr["st"]
    loads["k"].wait()
    loads["v"].wait()
    for h in range(heads):
        down = down_all[:, h : h + 1]
        total = down[tokens - 1 : tokens]
        key = silu(lk[:, lanes(h)].astype(jnp.float32)).astype(jnp.bfloat16)
        lk[:, lanes(h)] = key
        faded = key.astype(jnp.float32) * jnp.exp(total - down)
        high = faded.astype(jnp.bfloat16)
        low = (faded - high.astype(jnp.float32)).astype(jnp.bfloat16)
        value = lv[:, lanes(h)]
        state = lax.dot_general(high, value, TN, preferred_element_type=jnp.float32)
        state += lax.dot_general(low, value, TN, preferred_element_type=jnp.float32)
        st[h // 2, pl.ds((h % 2) * HD, HD)] = state
        st[h // 2, pl.ds(2 * HD + h % 2, 1)] = jnp.broadcast_to(total, (1, HD))

    yall, rz, tz, zr, zt = scr["yall"], scr["rz"], scr["tz"], scr["zr"], scr["zt"]
    ez, er, eq, pre, ent = scr["ez"], scr["er"], scr["eq"], scr["pre"], scr["ent"]

    def wanted(source, zz, yy):
        block = 2 * (zz * NY + yy)
        return jnp.maximum(sel_ref[source, block], sel_ref[source, block + 1])

    stage, far = scr["stage"], scr["far"]
    picks, selves = [], []

    def pick(n, offset, refs, kinds):
        source = zplus(offset) * NY + y
        for r in range(NY):
            spot = wanted(source, z, yplus(r))
            for kind in kinds:
                stage[n, r, kind] = refs[kind][spot]
        out = []
        for r in range(NY):
            for kind in kinds if len(kinds) == 1 else (None,):
                a, b, c = stage.at[n, r], fin_ref.at[source], 0
                if kind is not None:
                    a, b, c = a.at[kind], b.at[kind], kind
                if r == 0:
                    made = pltpu.make_async_copy(a, b, scr["self_s"].at[n, c])
                    made.start()
                    selves.append(made)
                    continue
                out.append(
                    copy(
                        a,
                        b,
                        scr["pick_s"].at[n, r - 1, c],
                        scr["pick_r"].at[n, r - 1, c],
                        at(z, yplus(r)),
                    )
                )
        picks.extend(out)
        return out

    def pick_far(sign, kind):
        k = 0 if sign > 0 else 1
        source = zplus(NZ - LAST * sign) * NY + y
        out = []
        for beyond in (1, 2):
            to = zplus(NZ + sign * beyond)
            for r in range(NY):
                if beyond == 2 and (r < 2) != (sign > 0):
                    continue
                spot = wanted(source, to, yplus(r))
                far[k, beyond - 1, r, kind] = bufs[sign, LAST][kind][spot]
                out.append(
                    copy(
                        far.at[k, beyond - 1, r, kind],
                        fin_ref.at[source, kind],
                        scr["far_s"].at[k, beyond - 1, r, kind],
                        scr["far_r"].at[k, beyond - 1, r, kind],
                        at(to, yplus(r)),
                    )
                )
        picks.extend(out)
        return out

    hold = {}

    def send_states():
        hold["ya"] = []
        for r in range(1, NY):
            made = copy(
                st.at[yplus(r)],
                yall.at[y],
                scr["ya_s"].at[r - 1],
                scr["ya_r"].at[r - 1],
                at(z, yplus(r)),
            )
            made.start()
            hold["ya"].append(made)

    def row_totals():
        yall[y] = st[y]
        for made in hold["ya"]:
            made.wait_recv()
        for hh in range(2):
            rows = pl.ds(hh * HD, HD)
            total = jnp.zeros((1, HD), jnp.float32)
            state = jnp.zeros((HD, HD), jnp.float32)
            for k in range(NY):
                if k > 0:
                    pre[k, rows] = state
                    pre[k, pl.ds(2 * HD + hh, 1)] = total
                step = yall[k, pl.ds(2 * HD + hh, 1)]
                state = jnp.exp(step) * state + yall[k, rows]
                total = total + step
            tz[hh] = total
            rz[pl.ds(hh * 8, 8)] = state.astype(jnp.bfloat16).reshape(8, 16, HD)

    def send_totals():
        hold["za"] = []
        for r in range(1, NZ):
            to = zplus(r)
            one = copy(rz.at[to], zr.at[z], scr["za_s"].at[r - 1], scr["za_r"].at[r - 1], at(to, y))
            two = copy(
                tz.at[to // 8], zt.at[z], scr["zb_s"].at[r - 1], scr["zb_r"].at[r - 1], at(to, y)
            )
            one.start()
            two.start()
            hold["za"] += [one, two]
        zr[z] = rz[z]
        zt[z] = tz[z // 8]

    def scan():
        for made in hold["za"]:
            made.wait_recv()
        state = jnp.zeros((16, HD), jnp.float32)
        for k in range(NZ):
            ez[k] = state.astype(jnp.bfloat16)
            state = jnp.exp(zt[k]) * state + zr[k].astype(jnp.float32)

    def send_entering():
        hold["zc"] = []
        for r in range(1, NZ):
            to = zplus(r)
            one = copy(ez.at[to], er.at[z], scr["zc_s"].at[r - 1], scr["zc_r"].at[r - 1], at(to, y))
            one.start()
            hold["zc"].append(one)
        er[z] = ez[z]

    def members():
        for made in hold["zc"]:
            made.wait_recv()
        row = er[...].astype(jnp.float32).reshape(2 * HD, HD)
        eq[0] = row
        for k in range(1, NY):
            for hh in range(2):
                rows = pl.ds(hh * HD, HD)
                faded = jnp.exp(pre[k, pl.ds(2 * HD + hh, 1)]) * row[hh * HD : (hh + 1) * HD]
                eq[k, rows] = faded + pre[k, rows]

    def send_members():
        hold["yb"] = []
        for r in range(1, NY):
            to = yplus(r)
            one = copy(eq.at[to], ent.at[y], scr["yb_s"].at[r - 1], scr["yb_r"].at[r - 1], at(z, to))
            one.start()
            hold["yb"].append(one)
        ent[y] = eq[y]

    attn = scr["attn"]

    def intra(h):
        if h == 0:
            loads["q"].wait()
        query = silu(lq[:, lanes(h)].astype(jnp.float32)).astype(jnp.bfloat16)
        lq[:, lanes(h)] = query
        scores = lax.dot_general(query, lk[:, lanes(h)], NT, preferred_element_type=jnp.float32)
        gaps = down_all[:, h : h + 1] - across_all[h : h + 1, :]
        t = lax.broadcasted_iota(jnp.int32, (tokens, tokens), 0)
        u = lax.broadcasted_iota(jnp.int32, (tokens, tokens), 1)
        weight = jnp.where(u <= t, jnp.exp(jnp.minimum(gaps, 0.0)), 0.0)
        attn[:, lanes(h)] = jnp.dot(
            (scores * weight).astype(jnp.bfloat16), lv[:, lanes(h)], preferred_element_type=jnp.float32
        )

    squares, norms = scr["squares"], scr["norms"]

    def inter(h):
        state = ent[h // 2, pl.ds((h % 2) * HD, HD)]
        high = state.astype(jnp.bfloat16)
        low = (state - high.astype(jnp.float32)).astype(jnp.bfloat16)
        query = lq[:, lanes(h)]
        moved = jnp.dot(query, high, preferred_element_type=jnp.float32)
        moved += jnp.dot(query, low, preferred_element_type=jnp.float32)
        whole = attn[:, lanes(h)] + jnp.exp(down_all[:, h : h + 1]) * moved
        attn[:, lanes(h)] = whole
        squares[...] = whole * whole if h == 0 else squares[...] + whole * whole

    def send_squares():
        norms[0] = lax.dot_general(
            jnp.ones((8, HD), jnp.float32),
            squares[...],
            NT,
            precision=HIGHEST,
            preferred_element_type=jnp.float32,
        )

    def start_squares():
        hold["sq"] = []
        for r in range(1, heads):
            one = copy(
                norms.at[0], norms.at[r], scr["sq_s"].at[r - 1], scr["sq_r"].at[r - 1], beside(r)
            )
            one.start()
            hold["sq"].append(one)

    def gate():
        for made in hold["sq"]:
            made.wait_recv()
        summed = norms[0]
        for r in range(1, heads):
            summed = summed + norms[r]
        first = jnp.where(lax.broadcasted_iota(jnp.int32, (8, HD), 0) == 0, 1.0, 0.0)
        tall = lax.dot_general(
            summed,
            first.astype(jnp.float32),
            TN,
            precision=HIGHEST,
            preferred_element_type=jnp.float32,
        )
        scaling = lax.rsqrt(tall / (QUERY_HEADS * HD) + 1e-06)
        loads["g"].wait()
        for h in range(heads):
            opened = 1.0 + jnp.exp(-lg[:, lanes(h)].astype(jnp.float32))
            shaped = attn[:, lanes(h)] * scaling * gain_ref[:, lanes(h)]
            lin_ref[:, lanes(h)] = (shaped / opened).astype(jnp.bfloat16)

    loads["ck"].wait()
    loads["cv"].wait()
    send_states()
    waiting = pick(0, 0, (own_k, own_v), (0, 1))
    tasks = {
        (1, 2): [row_totals],
        (1, 3): [spread, send_totals],
        (2, 0): [lambda: intra(0)],
        (2, 1): [lambda: intra(1)],
        (2, 2): [lambda: intra(2)],
        (2, 3): [lambda: intra(3)],
        (3, 1): [scan],
        (3, 2): [send_entering],
        (4, 0): [lambda: intra(4)],
        (4, 1): [lambda: intra(5)],
        (4, 2): [lambda: intra(6)],
        (4, 3): [lambda: intra(7)],
        (5, 1): [members],
        (5, 2): [send_members],
    }
    for d in range(1, LAST + 1):
        for c in range(CHUNKS):
            for sign in (1, -1):
                ring[sign, d, c].wait_recv()
                if d < LAST:
                    send_ring(sign, d + 1, c)
            for made in waiting:
                made.start()
            waiting = []
            quarter, rest = divmod((c + 1) * 4, CHUNKS)
            for task in tasks.get((d, quarter - 1), []) if rest == 0 else []:
                task()
            if d == LAST and 2 * (c + 1) % CHUNKS == 0:
                kind = c * 2 // CHUNKS
                waiting = pick_far(1, kind) + pick_far(-1, kind)
                waiting += pick(2 * d - 1, NZ - d, bufs[1, d], (kind,))
                waiting += pick(2 * d, d, bufs[-1, d], (kind,))
        if d < LAST:
            waiting = pick(2 * d - 1, NZ - d, bufs[1, d], (0, 1))
            waiting += pick(2 * d, d, bufs[-1, d], (0, 1))
    for made in waiting:
        made.start()
    for made in hold["yb"]:
        made.wait_recv()
    for h in range(heads):
        inter(h)
    send_squares()
    start_squares()
    gate()
    for made in picks:
        made.wait_recv()
    for made in selves:
        made.wait()
    for made in sends:
        made.wait_send()


def exchange(sel, ck, cv, lq, lk, lv, lg, ld, gain):
    tokens, width = lq.shape
    shards = 2 * LAST + 1
    dma = pltpu.SemaphoreType.DMA
    names = {
        "bufs": [pltpu.VMEM((8, BLOCK, HD), jnp.bfloat16)] * (4 * LAST),
        "own_k": pltpu.VMEM((8, BLOCK, HD), jnp.bfloat16),
        "own_v": pltpu.VMEM((8, BLOCK, HD), jnp.bfloat16),
        "stage": pltpu.VMEM((shards, NY, 2, BLOCK, HD), jnp.bfloat16),
        "far": pltpu.VMEM((2, 2, NY, 2, BLOCK, HD), jnp.bfloat16),
        "lq": pltpu.VMEM((tokens, width), jnp.bfloat16),
        "lk": pltpu.VMEM((tokens, width), jnp.bfloat16),
        "lv": pltpu.VMEM((tokens, width), jnp.bfloat16),
        "lg": pltpu.VMEM((tokens, width), jnp.bfloat16),
        "attn": pltpu.VMEM((tokens, width), jnp.float32),
        "squares": pltpu.VMEM((tokens, HD), jnp.float32),
        "norms": pltpu.VMEM((8, 8, tokens), jnp.float32),
        "down": pltpu.VMEM((tokens, 8), jnp.float32),
        "across": pltpu.VMEM((8, tokens), jnp.float32),
        "st": pltpu.VMEM((NY, 264, HD), jnp.float32),
        "yall": pltpu.VMEM((NY, 264, HD), jnp.float32),
        "pre": pltpu.VMEM((NY, 264, HD), jnp.float32),
        "rz": pltpu.VMEM((NZ, 16, HD), jnp.bfloat16),
        "tz": pltpu.VMEM((2, 1, HD), jnp.float32),
        "zr": pltpu.VMEM((NZ, 16, HD), jnp.bfloat16),
        "zt": pltpu.VMEM((NZ, 1, HD), jnp.float32),
        "ez": pltpu.VMEM((NZ, 16, HD), jnp.bfloat16),
        "er": pltpu.VMEM((NZ, 16, HD), jnp.bfloat16),
        "eq": pltpu.VMEM((NY, 256, HD), jnp.float32),
        "ent": pltpu.VMEM((NY, 256, HD), jnp.float32),
        "near": pltpu.SemaphoreType.REGULAR((2,)),
        "in_s": dma((6,)),
        "ring_s": dma((2, LAST, CHUNKS)),
        "ring_r": dma((2, LAST, CHUNKS)),
        "pick_s": dma((shards, NY - 1, 2)),
        "pick_r": dma((shards, NY - 1, 2)),
        "self_s": dma((shards, 2)),
        "far_s": dma((2, 2, NY, 2)),
        "far_r": dma((2, 2, NY, 2)),
        "ya_s": dma((NY - 1,)),
        "ya_r": dma((NY - 1,)),
        "yb_s": dma((NY - 1,)),
        "yb_r": dma((NY - 1,)),
        "za_s": dma((NZ - 1,)),
        "za_r": dma((NZ - 1,)),
        "zb_s": dma((NZ - 1,)),
        "zb_r": dma((NZ - 1,)),
        "zc_s": dma((NZ - 1,)),
        "zc_r": dma((NZ - 1,)),
        "sq_s": dma((7,)),
        "sq_r": dma((7,)),
    }
    flat, tree = jax.tree.flatten(names, is_leaf=lambda leaf: not isinstance(leaf, (dict, list)))

    def body(*refs):
        exchange_kernel(*refs[:11], jax.tree.unflatten(tree, refs[11:]))

    vmem = pl.BlockSpec(memory_space=pltpu.VMEM)
    hbm = pl.BlockSpec(memory_space=pltpu.HBM)
    return pl.pallas_call(
        body,
        out_shape=(
            jax.ShapeDtypeStruct((NZ * NY, 2, BLOCK, HD), jnp.bfloat16),
            jax.ShapeDtypeStruct((tokens, width), jnp.bfloat16),
        ),
        in_specs=[pl.BlockSpec(memory_space=pltpu.SMEM)] + [hbm] * 6 + [vmem] * 2,
        out_specs=(hbm, vmem),
        scratch_shapes=flat,
        compiler_params=pltpu.CompilerParams(
            collective_id=0, has_side_effects=True, vmem_limit_bytes=VMEM_LIMIT
        ),
        name="exchange",
    )(sel, ck, cv, lq, lk, lv, lg, ld, gain)


GROUP = 4


def attend_kernel(lists_ref, counts_ref, q_ref, sk_ref, sv_ref, fin_ref, out_ref, qs, keys, values, sc, top, tot, acc):
    me = lax.axis_index("ctx")
    factor = math.log2(math.e) / math.sqrt(HD)
    heads = q_ref.shape[1] // HD
    selected = lists_ref.shape[0]
    rows = heads * BLOCK
    chunk = BLOCK
    wide = GROUP * BLOCK

    def parts(full):
        return [full[:, i * BLOCK : (i + 1) * BLOCK] for i in range(GROUP)]

    for qb in range(2):
        tokens = pl.ds(qb * BLOCK, BLOCK)
        query_block = 2 * me + qb
        own = qb + 1
        for g in range(heads):
            qs[pl.ds(g * BLOCK, BLOCK)] = q_ref[tokens, g * HD : (g + 1) * HD]
        keys[0:BLOCK] = sk_ref[tokens]
        values[0:BLOCK] = sv_ref[tokens]
        if qb == 1:
            keys[BLOCK : 2 * BLOCK] = sk_ref[0:BLOCK]
            values[BLOCK : 2 * BLOCK] = sv_ref[0:BLOCK]
        for j in range(selected):
            source = lists_ref[j, query_block] >> 3
            place = pl.ds((own + j) * BLOCK, BLOCK)
            keys[place] = fin_ref[source, 0]
            values[place] = fin_ref[source, 1]
        if own + selected < 5 * GROUP:
            place = pl.ds((own + selected) * BLOCK, (5 * GROUP - own - selected) * BLOCK)
            keys[place] = jnp.zeros(((5 * GROUP - own - selected) * BLOCK, HD), jnp.bfloat16)
            values[place] = jnp.zeros(((5 * GROUP - own - selected) * BLOCK, HD), jnp.bfloat16)
        filled = (own + counts_ref[query_block]) * BLOCK

        def score(n, first):
            base = 0 if first else pl.multiple_of(n * wide, wide)
            these = keys[pl.ds(base, wide)]
            for at in range(0, rows, chunk):
                part = pl.ds(at, chunk)
                s = lax.dot_general(qs[part], these, NT, preferred_element_type=jnp.float32)
                u = lax.broadcasted_iota(jnp.int32, (chunk, wide), 1)
                keep = u < filled - base
                if first:
                    t = lax.broadcasted_iota(jnp.int32, (chunk, wide), 0)
                    keep = keep & ((u <= t) | (u >= BLOCK))
                s = jnp.where(keep, s, -1e30)
                sc[n, part] = s
                most = functools.reduce(jnp.maximum, parts(s))
                top[part] = most if first else jnp.maximum(top[part], most)

        def mix(n, first):
            base = 0 if first else pl.multiple_of(n * wide, wide)
            these = values[pl.ds(base, wide)]
            for at in range(0, rows, chunk):
                part = pl.ds(at, chunk)
                peak = top[part]
                w = [jnp.exp2(s * factor - peak) for s in parts(sc[n, part])]
                m = jnp.dot(
                    jnp.concatenate([piece.astype(jnp.bfloat16) for piece in w], axis=1),
                    these,
                    preferred_element_type=jnp.float32,
                )
                some = functools.reduce(jnp.add, w)
                tot[part] = some if first else tot[part] + some
                acc[part] = m if first else acc[part] + m

        def body(step):
            def run(n, carry):
                step(n, False)
                return carry

            return run

        groups = (filled + wide - 1) // wide
        score(0, True)
        lax.fori_loop(1, groups, body(score), 0)
        for at in range(0, rows, chunk):
            part = pl.ds(at, chunk)
            top[part] = jnp.broadcast_to(
                jnp.max(top[part], axis=1, keepdims=True) * factor, (chunk, BLOCK)
            )
        mix(0, True)
        lax.fori_loop(1, groups, body(mix), 0)
        for g in range(heads):
            part = pl.ds(g * BLOCK, BLOCK)
            whole = jnp.sum(tot[part], axis=1, keepdims=True)
            out_ref[tokens, g * HD : (g + 1) * HD] = (acc[part] / whole).astype(jnp.bfloat16)


def attend(lists, counts, queries, keys, values, fin):
    tok_rows, width = queries.shape
    rows = width // HD * BLOCK
    vmem = pl.BlockSpec(memory_space=pltpu.VMEM)
    smem = pl.BlockSpec(memory_space=pltpu.SMEM)
    return pl.pallas_call(
        attend_kernel,
        out_shape=jax.ShapeDtypeStruct((tok_rows, width), jnp.bfloat16),
        in_specs=[smem, smem, vmem, vmem, vmem, vmem],
        out_specs=vmem,
        scratch_shapes=[
            pltpu.VMEM((rows, HD), jnp.bfloat16),
            pltpu.VMEM((5 * GROUP * BLOCK, HD), jnp.bfloat16),
            pltpu.VMEM((5 * GROUP * BLOCK, HD), jnp.bfloat16),
            pltpu.VMEM((5, rows, GROUP * BLOCK), jnp.float32),
            pltpu.VMEM((rows, BLOCK), jnp.float32),
            pltpu.VMEM((rows, BLOCK), jnp.float32),
            pltpu.VMEM((rows, HD), jnp.float32),
        ],
        compiler_params=pltpu.CompilerParams(vmem_limit_bytes=VMEM_LIMIT),
        name="attend",
    )(lists, counts, queries, keys, values, fin)


def table(lists, counts):
    entry = jnp.arange(lists.shape[0], dtype=jnp.int32)[:, None]
    flat = jnp.where(entry < counts[None, :], lists, -1)
    owners = jnp.arange(NZ * NY, dtype=jnp.int32)
    hit = (flat >> 3)[:, None, :] == owners[None, :, None]
    return jnp.max(jnp.where(hit, (flat & 7)[:, None, :], 0), axis=0)


def local(
    lin_queries,
    lin_keys,
    lin_values,
    log_decay,
    lin_gate,
    norm_gain,
    soft_queries,
    slab_keys,
    slab_values,
    cache_keys,
    cache_values,
    block_lists,
    live_counts,
):
    blocks = cache_keys.shape[0] // BLOCK
    fin, lin_out = exchange(
        table(block_lists.T, live_counts),
        cache_keys.reshape(blocks, BLOCK, HD),
        cache_values.reshape(blocks, BLOCK, HD),
        lin_queries,
        lin_keys,
        lin_values,
        lin_gate,
        log_decay.T,
        norm_gain.reshape(1, -1),
    )
    soft_out = attend(block_lists.T, live_counts, soft_queries, slab_keys, slab_values, fin)
    return (lin_out, soft_out)


def solution(mesh):
    in_specs = (
        P("ctx", "head"),
        P("ctx", "head"),
        P("ctx", "head"),
        P("ctx", "head"),
        P("ctx", "head"),
        P("head"),
        P("ctx", "head"),
        P("ctx", "head"),
        P("ctx", "head"),
        P("ctx", "head"),
        P("ctx", "head"),
        P(),
        P(),
    )
    out_specs = (P("ctx", "head"), P("ctx", "head"))
    return jax.shard_map(local, mesh=mesh, in_specs=in_specs, out_specs=out_specs, check_vma=False)
```
